32 devices in a mesh: gx: 8 (over y, x, core), gy: 4 (over z).
Axes of the slice: x: 2, y: 2, z: 4, core: 2. Of those that a mesh axis runs over, the one named last changes fastest.
Arguments:
- fields: bfloat16 [128, 128, 256], P('gx', 'gy'), may hold values from -6 to 6
- w_down: bfloat16 [3, 3, 3, 32, 32], replicated, may hold values from -0.21875 to 0.21875
- w_pool: bfloat16 [2, 2, 2, 32, 64], replicated, may hold values from -0.375 to 0.375
- w_mid: bfloat16 [3, 3, 3, 64, 64], replicated, may hold values from -0.15625 to 0.15625
- w_unpool: bfloat16 [2, 2, 2, 64, 32], replicated, may hold values from -0.75 to 0.75
- w_up: bfloat16 [3, 3, 3, 32, 32], replicated, may hold values from -0.21875 to 0.21875
- cotangent: bfloat16 [128, 128, 256], P('gx', 'gy'), may hold values from -6 to 6
Outputs:
- output: bfloat16 [128, 128, 256], P('gx', 'gy')
- grad_fields: bfloat16 [128, 128, 256], P('gx', 'gy')
- grad_down: float32 [3, 3, 3, 32, 32], replicated
- grad_pool: float32 [2, 2, 2, 32, 64], replicated
- grad_mid: float32 [3, 3, 3, 64, 64], replicated
- grad_unpool: float32 [2, 2, 2, 64, 32], replicated
- grad_up: float32 [3, 3, 3, 32, 32], replicated
The draws below stay inside these ranges and needn't reach their ends.
All inputs are finite; a program needn't handle non-finite values.
Results may differ from the reference program's by a relative error of at most 0.0071.
Values may be sent and summed in bfloat16 or wider, within the bound.
A program may use at most 128 MiB of HBM per device.

```python
import math
import jax
import jax.numpy as jnp
from jax import lax

CF = 32
CC = 64
ZS = 8
NX = 128
NY = 128


def levels(stream_key, extent, split, low, high):
    def one(dim, shards_of):
        heights = jax.random.uniform(jax.random.fold_in(jax.random.fold_in(stream_key, 6), dim), (shards_of,), jnp.float32, low / len(split), high / len(split))
        return jnp.repeat(jnp.exp(heights), extent[dim] // shards_of).reshape((-1,) + (1,) * (len(extent) - dim - 1))

    level = one(*split[0])
    for cut in split[1:]:
        level = level * one(*cut)
    return level


def bell_draw(own_key, extent, scale, reach, cuts=(), held_as=jnp.bfloat16):
    result = jax.random.normal(own_key, extent, jnp.float32) * scale
    if len(cuts) > 0:
        result = levels(own_key, extent, cuts, -0.22, 0.18) * result
    return jnp.clip(result, min=-reach, max=reach).astype(held_as)


def setup_inputs(seed: int = 0) -> dict:
    key_of = jax.random.split(jax.random.key(seed), 8)
    return {
        "fields": bell_draw(key_of[0], (NX, NY, ZS * CF), 1.0, 6.0, ((0, 8), (1, 4))),
        "w_down": bell_draw(key_of[1], (3, 3, 3, CF, CF), (27 * CF) ** -0.5, 0.21875),
        "w_pool": bell_draw(key_of[2], (2, 2, 2, CF, CC), (8 * CF) ** -0.5, 0.375),
        "w_mid": bell_draw(key_of[3], (3, 3, 3, CC, CC), (27 * CC) ** -0.5, 0.15625),
        "w_unpool": bell_draw(key_of[4], (2, 2, 2, CC, CF), CC ** -0.5, 0.75),
        "w_up": bell_draw(key_of[5], (3, 3, 3, CF, CF), (27 * CF) ** -0.5, 0.21875),
        "cotangent": bell_draw(key_of[6], (NX, NY, ZS * CF), 1.0, 6.0, ((0, 8), (1, 4))),
    }


def dsilu(value):
    sig = jax.nn.sigmoid(value)
    return sig * (1.0 + value * (1.0 - sig))

def plane_shifts(planes):
    return jnp.stack([jnp.eye(planes, k=1 - kk, dtype=jnp.float32) for kk in range(3)])

def band_matrix(weight, planes):
    shifts = plane_shifts(planes)
    band = jnp.einsum('kpz,abkco->abpczo', shifts, weight.astype(jnp.float32))
    return band.reshape(3, 3, planes * weight.shape[3], planes * weight.shape[4]).astype(jnp.bfloat16)

def band_to_weight(dband, planes, cin, cout):
    shifts = plane_shifts(planes)
    return jnp.einsum('kpz,abpczo->abkco', shifts, dband.reshape(3, 3, planes, cin, planes, cout))

def flipped(weight):
    return jnp.transpose(weight[::-1, ::-1, ::-1], (0, 1, 2, 4, 3))

def wrap_pad(field):
    return jnp.pad(field, ((1, 1), (1, 1), (0, 0)), mode='wrap')

def conv_whole(field, weight, planes):
    band = band_matrix(weight, planes)
    padded = wrap_pad(field)
    xs, ys, width = field.shape
    total = jnp.zeros((xs * ys, band.shape[3]), jnp.float32)
    for aa in range(3):
        for bb in range(3):
            piece = padded[aa:aa + xs, bb:bb + ys, :].reshape(xs * ys, width)
            total = total + jnp.dot(piece, band[aa, bb], preferred_element_type=jnp.float32)
    return total.reshape(xs, ys, -1)

def conv_weight_grad(field, dout, planes, cin, cout):
    padded = wrap_pad(field)
    xs, ys, width = field.shape
    flat = dout.reshape(xs * ys, -1)
    parts = []
    for aa in range(3):
        for bb in range(3):
            piece = padded[aa:aa + xs, bb:bb + ys, :].reshape(xs * ys, width)
            parts.append(lax.dot_general(piece, flat, (((0,), (0,)), ((), ())), preferred_element_type=jnp.float32))
    return band_to_weight(jnp.stack(parts), planes, cin, cout)

def split_fine(field):
    xs, ys, width = field.shape
    parts = field.reshape(xs // 2, 2, ys // 2, 2, width).transpose(0, 2, 1, 3, 4)
    return parts.reshape(xs // 2 * (ys // 2), 4 * width)

def merge_fine(flat, xs, ys):
    width = flat.shape[1] // 4
    return flat.reshape(xs // 2, ys // 2, 2, 2, width).transpose(0, 2, 1, 3, 4).reshape(xs, ys, width)

def pool_matrix(weight, half):
    eye = jnp.eye(half, dtype=jnp.float32)
    mat = jnp.einsum('yz,ijlco->ijylczo', eye, weight.astype(jnp.float32))
    return mat.reshape(-1, half * weight.shape[4]).astype(jnp.bfloat16)

def unpool_matrix(weight, half):
    eye = jnp.eye(half, dtype=jnp.float32)
    mat = jnp.einsum('yz,ijlof->yoijzlf', eye, weight.astype(jnp.float32))
    return mat.reshape(half * weight.shape[3], -1).astype(jnp.bfloat16)

def reference(fields, w_down, w_pool, w_mid, w_unpool, w_up, cotangent):
    cf = w_down.shape[3]
    cc = w_mid.shape[3]
    xs, ys = (fields.shape[0], fields.shape[1])
    half = ZS // 2
    pmat = pool_matrix(w_pool, half)
    umat = unpool_matrix(w_unpool, half)
    pre_down = conv_whole(fields, w_down, ZS)
    hidden = jax.nn.silu(pre_down).astype(jnp.bfloat16)
    hidden_parts = split_fine(hidden)
    pre_pool = jnp.dot(hidden_parts, pmat, preferred_element_type=jnp.float32).reshape(xs // 2, ys // 2, -1)
    coarse = jax.nn.silu(pre_pool).astype(jnp.bfloat16)
    pre_mid = conv_whole(coarse, w_mid, half)
    middle = (coarse.astype(jnp.float32) + jax.nn.silu(pre_mid)).astype(jnp.bfloat16)
    middle_flat = middle.reshape(-1, middle.shape[2])
    lifted = jnp.dot(middle_flat, umat, preferred_element_type=jnp.float32)
    pre_up = hidden.astype(jnp.float32) + merge_fine(lifted, xs, ys)
    skip = jax.nn.silu(pre_up).astype(jnp.bfloat16)
    output = (fields.astype(jnp.float32) + conv_whole(skip, w_up, ZS)).astype(jnp.bfloat16)
    d_up = (conv_whole(cotangent, flipped(w_up), ZS) * dsilu(pre_up)).astype(jnp.bfloat16)
    d_up_parts = split_fine(d_up)
    d_middle = lax.dot_general(d_up_parts, umat, (((1,), (1,)), ((), ())), preferred_element_type=jnp.float32)
    d_middle = d_middle.reshape(xs // 2, ys // 2, -1)
    d_mid = (d_middle * dsilu(pre_mid)).astype(jnp.bfloat16)
    d_coarse = d_middle + conv_whole(d_mid, flipped(w_mid), half)
    d_pool = (d_coarse * dsilu(pre_pool)).astype(jnp.bfloat16)
    d_pool_flat = d_pool.reshape(-1, d_pool.shape[2])
    back = lax.dot_general(d_pool_flat, pmat, (((1,), (1,)), ((), ())), preferred_element_type=jnp.float32)
    d_hidden = d_up.astype(jnp.float32) + merge_fine(back, xs, ys)
    d_down = (d_hidden * dsilu(pre_down)).astype(jnp.bfloat16)
    grad_fields = (cotangent.astype(jnp.float32) + conv_whole(d_down, flipped(w_down), ZS)).astype(jnp.bfloat16)
    scale = 1.0 / math.sqrt(xs * ys * ZS)
    grad_up = conv_weight_grad(skip, cotangent, ZS, cf, cf) * scale
    grad_mid = conv_weight_grad(coarse, d_mid, half, cc, cc) * scale
    grad_down = conv_weight_grad(fields, d_down, ZS, cf, cf) * scale
    eye = jnp.eye(half, dtype=jnp.float32)
    d_umat = lax.dot_general(middle_flat, d_up_parts, (((0,), (0,)), ((), ())), preferred_element_type=jnp.float32)
    grad_unpool = jnp.einsum('yz,yoijzlf->ijlof', eye, d_umat.reshape(half, cc, 2, 2, half, 2, cf)) * scale
    d_pmat = lax.dot_general(hidden_parts, d_pool_flat, (((0,), (0,)), ((), ())), preferred_element_type=jnp.float32)
    grad_pool = jnp.einsum('yz,ijylczo->ijlco', eye, d_pmat.reshape(2, 2, half, 2, cf, half, cc)) * scale
    return (output, grad_fields, grad_down, grad_pool, grad_mid, grad_unpool, grad_up)
```

```python
import math

import jax
import jax.numpy as jnp
from jax import lax
from jax.sharding import PartitionSpec as P


def padded_2(block, sides, width):
    for axis, dim in sides:
        count = lax.axis_size(axis)
        forward = [(i, i + 1) for i in range(count - 1)]
        forward.append((count - 1, 0))
        backward = [(target, source) for source, target in forward]
        low = lax.ppermute(
            lax.slice_in_dim(block, block.shape[dim] - width, None, axis=dim), axis, forward
        )
        high = lax.ppermute(lax.slice_in_dim(block, 0, width, axis=dim), axis, backward)
        block = jnp.concatenate([low, block, high], axis=dim)
    return block


def dsilu(value):
    sig = jax.nn.sigmoid(value)
    return sig * (1.0 + value * (1.0 - sig))


def plane_shifts(planes):
    return jnp.stack([jnp.eye(planes, k=1 - kk, dtype=jnp.float32) for kk in range(3)])


def widened(weight, copies):
    cout = weight.shape[-1]
    tiled = jnp.tile(jnp.eye(cout, dtype=weight.dtype), (1, copies))
    wide = jnp.dot(weight.reshape(-1, cout), tiled, preferred_element_type=jnp.float32)
    return wide.astype(jnp.bfloat16).reshape(weight.shape[:-1] + (copies * cout,))


def lane_offset(planes, cout):
    lanes = lax.broadcasted_iota(jnp.int32, (planes, 1, planes * cout), 2) // cout
    return lanes - lax.broadcasted_iota(jnp.int32, (planes, 1, planes * cout), 0)


def band_matrix(weight, planes):
    cin, cout = weight.shape[3], weight.shape[4]
    wide = widened(weight, planes)
    offset = lane_offset(planes, cout)
    band = jnp.zeros((3, 3, planes, cin, planes * cout), jnp.bfloat16)
    for kk in range(3):
        band = jnp.where(offset == 1 - kk, wide[:, :, kk][:, :, None], band)
    return band.reshape(9 * planes * cin, planes * cout)


def band_to_weight(dband, planes, cin, cout):
    shifts = plane_shifts(planes)
    return jnp.einsum("kpz,abpczo->abkco", shifts, dband.reshape(3, 3, planes, cin, planes, cout))


def flipped(weight):
    return jnp.transpose(weight[::-1, ::-1, ::-1], (0, 1, 2, 4, 3))


def fine_rim(field):
    return padded_2(field, (("gx", 0), ("gy", 1)), 1)


def coarse_rim(field):
    return padded_2(field, (("gx", 0), ("gy", 1)), 1)


def columns(padded):
    xs = padded.shape[0] - 2
    ys = padded.shape[1] - 2
    cols = jnp.concatenate(
        [padded[aa : aa + xs, bb : bb + ys, :] for aa in range(3) for bb in range(3)], axis=2
    )
    return cols.reshape(xs * ys, -1)


def conv_padded(padded, band):
    xs = padded.shape[0] - 2
    ys = padded.shape[1] - 2
    return jnp.dot(columns(padded), band, preferred_element_type=jnp.float32).reshape(xs, ys, -1)


def weight_grad(padded, dout, planes, cin, cout):
    flat = dout.reshape(-1, dout.shape[2])
    dband = lax.dot_general(
        columns(padded), flat, (((0,), (0,)), ((), ())), preferred_element_type=jnp.float32
    )
    return band_to_weight(dband, planes, cin, cout)


def split_fine(field):
    xs, ys, width = field.shape
    parts = field.reshape(xs // 2, 2, ys // 2, 2, width).transpose(0, 2, 1, 3, 4)
    return parts.reshape(xs // 2 * (ys // 2), 4 * width)


def merge_fine(flat, xs, ys):
    width = flat.shape[1] // 4
    return (
        flat.reshape(xs // 2, ys // 2, 2, 2, width).transpose(0, 2, 1, 3, 4).reshape(xs, ys, width)
    )


def pool_matrix(weight, half):
    cout = weight.shape[4]
    wide = widened(weight, half)
    offset = lane_offset(half, cout)[:, None]
    mat = jnp.where(offset == 0, wide[:, :, None], jnp.zeros((), jnp.bfloat16))
    return mat.reshape(-1, half * cout)


def summed_over(parts, axes, scale):
    count = 1
    for axis in axes:
        count *= lax.axis_size(axis)
    flat = jnp.concatenate([part.reshape(-1, 128) for part in parts], axis=0)
    rows = -(-flat.shape[0] // (8 * count)) * 8
    flat = jnp.pad(flat, ((0, rows * count - flat.shape[0]), (0, 0)))
    pieces = lax.all_to_all(flat.reshape(count, rows, 128), axes, 0, 0, tiled=True)
    whole = lax.all_gather(jnp.sum(pieces, axis=0) * scale, axes, axis=0, tiled=True)
    out, start = [], 0
    for part in parts:
        size = part.size // 128
        out.append(whole[start : start + size].reshape(part.shape))
        start += size
    return tuple(out)


def per_device(fields, w_down, w_pool, w_mid, w_unpool, w_up, cotangent):
    cf = w_down.shape[3]
    cc = w_mid.shape[3]
    xs, ys = (fields.shape[0], fields.shape[1])
    width = fields.shape[2]
    planes = width // cf
    half = planes // 2
    pmat = pool_matrix(w_pool, half)
    umat_t = pool_matrix(jnp.swapaxes(w_unpool, 3, 4), half)
    joined = padded_2(jnp.concatenate((fields, cotangent), axis=2), (("gx", 0), ("gy", 1)), 1)
    fields_pad = joined[:, :, :width]
    cot_pad = joined[:, :, width:]
    pre_down = conv_padded(fields_pad, band_matrix(w_down, planes))
    hidden = jax.nn.silu(pre_down).astype(jnp.bfloat16)
    hidden_parts = split_fine(hidden)
    pre_pool = jnp.dot(hidden_parts, pmat, preferred_element_type=jnp.float32).reshape(
        xs // 2, ys // 2, -1
    )
    coarse = jax.nn.silu(pre_pool).astype(jnp.bfloat16)
    coarse_pad = coarse_rim(coarse)
    pre_mid = conv_padded(coarse_pad, band_matrix(w_mid, half))
    middle = (coarse.astype(jnp.float32) + jax.nn.silu(pre_mid)).astype(jnp.bfloat16)
    middle_flat = middle.reshape(-1, middle.shape[2])
    lifted = lax.dot_general(
        middle_flat, umat_t, (((1,), (1,)), ((), ())), preferred_element_type=jnp.float32
    )
    pre_up = hidden.astype(jnp.float32) + merge_fine(lifted, xs, ys)
    skip = jax.nn.silu(pre_up).astype(jnp.bfloat16)
    skip_pad = fine_rim(skip)
    output = (fields.astype(jnp.float32) + conv_padded(skip_pad, band_matrix(w_up, planes))).astype(
        jnp.bfloat16
    )
    d_up = (conv_padded(cot_pad, band_matrix(flipped(w_up), planes)) * dsilu(pre_up)).astype(
        jnp.bfloat16
    )
    d_up_parts = split_fine(d_up)
    d_middle = jnp.dot(d_up_parts, umat_t, preferred_element_type=jnp.float32)
    d_middle = d_middle.reshape(xs // 2, ys // 2, -1)
    d_mid = (d_middle * dsilu(pre_mid)).astype(jnp.bfloat16)
    d_coarse = d_middle + conv_padded(coarse_rim(d_mid), band_matrix(flipped(w_mid), half))
    d_pool = (d_coarse * dsilu(pre_pool)).astype(jnp.bfloat16)
    d_pool_flat = d_pool.reshape(-1, d_pool.shape[2])
    back = lax.dot_general(
        d_pool_flat, pmat, (((1,), (1,)), ((), ())), preferred_element_type=jnp.float32
    )
    d_hidden = d_up.astype(jnp.float32) + merge_fine(back, xs, ys)
    d_down = (d_hidden * dsilu(pre_down)).astype(jnp.bfloat16)
    grad_fields = (
        cotangent.astype(jnp.float32)
        + conv_padded(fine_rim(d_down), band_matrix(flipped(w_down), planes))
    ).astype(jnp.bfloat16)
    part_up = weight_grad(skip_pad, cotangent, planes, cf, cf)
    part_mid = weight_grad(coarse_pad, d_mid, half, cc, cc)
    part_down = weight_grad(fields_pad, d_down, planes, cf, cf)
    eye = jnp.eye(half, dtype=jnp.float32)
    d_umat = lax.dot_general(
        middle_flat, d_up_parts, (((0,), (0,)), ((), ())), preferred_element_type=jnp.float32
    )
    part_unpool = jnp.einsum("yz,yoijzlf->ijlof", eye, d_umat.reshape(half, cc, 2, 2, half, 2, cf))
    d_pmat = lax.dot_general(
        hidden_parts, d_pool_flat, (((0,), (0,)), ((), ())), preferred_element_type=jnp.float32
    )
    part_pool = jnp.einsum("yz,ijylczo->ijlco", eye, d_pmat.reshape(2, 2, half, 2, cf, half, cc))
    scale = 1.0 / math.sqrt(xs * ys * planes * lax.axis_size("gx") * lax.axis_size("gy"))
    grad_down, grad_pool, grad_mid, grad_unpool, grad_up = summed_over(
        (part_down, part_pool, part_mid, part_unpool, part_up), ("gx", "gy"), scale
    )
    return (output, grad_fields, grad_down, grad_pool, grad_mid, grad_unpool, grad_up)


def solution(mesh):
    placed = (P("gx", "gy", None), P(), P(), P(), P(), P(), P("gx", "gy", None))
    return jax.shard_map(
        per_device,
        mesh=mesh,
        in_specs=placed,
        out_specs=(P("gx", "gy", None), P("gx", "gy", None), P(), P(), P(), P(), P()),
        check_vma=False,
    )
```
